512 devices in a mesh: row: 8 (over y), col: 16 (over x, z_hi, core), layer: 4 (over z_lo).
Axes of the slice: x: 4, y: 8, z: 8 (z_hi: 2, z_lo: 4; z = z_hi * 4 + z_lo), core: 2. Of those that a mesh axis runs over, the one named last changes fastest.
Arguments:
- sign_iterate: bfloat16 [8192, 8192], P('row', 'col'), may hold values from -0.109375 to 0.109375
- square: bfloat16 [8192, 8192], P('row', 'col'), may hold values from -6 to 6
- pattern: int32 [64, 64], replicated, may hold values 0 or 1
- keep: int32 [64, 64], replicated, may hold values from 0 to 1, as said below
Outputs:
- product: bfloat16 [8192, 8192], P(('row', 'layer'), 'col')
The draws below stay inside these ranges and needn't reach their ends.
Inputs may be any that keep to these rules, and one draw needn't show every extreme that they name: In every region of 2 block rows by 4 block columns, aligned to the output's shards along row+layer and col, exactly 6 blocks have keep 1.
All inputs are finite; a program needn't handle non-finite values.
Results may differ from the reference program's by a relative error of at most 0.001.
Values may be sent and summed in bfloat16 or wider, within the bound.
No kernel may reach another device: no remote copies, remote signals or barrier semaphores. Data moves between devices by JAX's collectives and lax.ppermute only.
A program may use at most 64 MiB of HBM per device.

```python
import jax
import jax.numpy as jnp

BLK = 128
ORDER = 8192
NB = 64
REGION_ROWS = 2
REGION_COLS = 4
KEPT = 6


def draw_keep(key, part):
    grid_rows = NB // REGION_ROWS
    grid_cols = NB // REGION_COLS
    count = REGION_ROWS * REGION_COLS
    subkey = jax.random.fold_in(key, 7)
    keys = jax.random.split(subkey, grid_rows * grid_cols)
    perms = jax.vmap(lambda k: jax.random.permutation(k, count))(keys)
    flags = (perms < KEPT).astype(jnp.int32)
    flags = flags.reshape(grid_rows, grid_cols, REGION_ROWS, REGION_COLS)
    return flags.transpose(0, 2, 1, 3).reshape(NB, NB)


def with_ends(entries, own_key, smallest, top_value):
    longest = entries.shape.index(max(entries.shape))
    spots = []
    for shift in (0, 1):
        where = [jax.random.randint(jax.random.fold_in(own_key, axis), (), 0, length) for axis, length in enumerate(entries.shape)]
        where[longest] = (where[longest] + shift) % entries.shape[longest]
        spots.append(tuple(where))
    return entries.at[spots[0]].set(smallest).at[spots[1]].set(top_value)


def levels(own_key, extent, cuts, low, top_value):
    def one(axis_at, blocks):
        draws = jax.random.uniform(jax.random.fold_in(jax.random.fold_in(own_key, 6), axis_at), (blocks,), jnp.float32, low / len(cuts), top_value / len(cuts))
        return jnp.repeat(jnp.exp(draws), extent[axis_at] // blocks).reshape((-1,) + (1,) * (len(extent) - axis_at - 1))

    factor_of = one(*cuts[0])
    for cut in cuts[1:]:
        factor_of = factor_of * one(*cut)
    return factor_of


def centred(stream_key, shape, scale, reach, cuts=(), kind=jnp.bfloat16):
    level = levels(stream_key, shape, cuts, -0.22, 0.18) if cuts else 1.0
    entries = jax.random.normal(stream_key, shape, jnp.float32) * scale * level
    return jnp.minimum(jnp.maximum(entries, -reach), reach).astype(kind)


def setup_inputs(seed: int = 0) -> dict:
    splits = jax.random.split(jax.random.key(seed), 5)
    sign_iterate = centred(splits[0], (ORDER, ORDER), (ORDER // 3) ** -0.5, 0.109375, ((0, 8), (1, 16)))
    square = centred(splits[1], (ORDER, ORDER), 1.0, 6.0, ((0, 8), (1, 16)))
    pattern = with_ends((jax.random.randint(splits[2], (NB, NB), 0, 3) < 1).astype(jnp.int32), jax.random.fold_in(splits[2], 1), 0, 1)
    keep = draw_keep(jax.random.fold_in(splits[4], 71), 0)
    return dict(sign_iterate=sign_iterate, square=square, pattern=pattern, keep=keep)


def apply_blocks(matrix, mask):
    nrow = mask.shape[0]
    ncol = mask.shape[1]
    shaped = matrix.reshape(nrow, BLK, ncol, BLK)
    chosen = (mask == 1)[:, None, :, None]
    return jnp.where(chosen, shaped, jnp.zeros_like(shaped)).reshape(matrix.shape)


def reference(sign_iterate, square, pattern, keep):
    stored = apply_blocks(sign_iterate, pattern)
    full = jnp.dot(stored, square, preferred_element_type=jnp.float32)
    return apply_blocks(full, keep).astype(jnp.bfloat16)
```

```python
import functools

import jax
import jax.numpy as jnp
from jax import lax
from jax.experimental import pallas as pl
from jax.experimental.pallas import tpu as pltpu
from jax.sharding import PartitionSpec as P

BLK = 128
AXES = ("row", "col", "layer")
ROWS, XS, LAYERS = 8, 4, 4
KEPT = 6
EXTRA = 16
LEVELS = 32000.0


def table(move):
    pairs = []
    for r in range(ROWS):
        for x in range(XS):
            for z in range(2):
                for k in range(2):
                    for l in range(LAYERS):
                        r2, x2, z2, k2, l2 = move(r, x, z, k, l)
                        here = (r * 16 + x * 4 + z * 2 + k) * LAYERS + l
                        there = ((r2 % ROWS) * 16 + (x2 % XS) * 4 + z2 * 2 + k2) * LAYERS + l2
                        pairs.append((here, there))
    return pairs


ALONG_Y = table(lambda r, x, z, k, l: (r + 1 - 2 * k, x, z, k, l))
ALONG_X = table(lambda r, x, z, k, l: (r, x + 1 - 2 * k, z, k, l))
ACROSS_Z = table(lambda r, x, z, k, l: (r, x, 1 - z, k, l ^ 2))
OTHER_CORE = table(lambda r, x, z, k, l: (r, x, z, 1 - k, l))
CORE_PAIRS = [[2 * i, 2 * i + 1] for i in range(8)]


def send(value, pairs):
    return lax.ppermute(value, AXES, pairs)


def both_cores(value):
    return lax.all_gather(value, "col", axis=0, tiled=False, axis_index_groups=CORE_PAIRS)


def product_kernel(
    at_ref, mask_ref, keep_ref,
    x0_ref, x1_ref, x1o_ref, x2_ref, x2o_ref,
    s0_ref, s1_ref, s2_ref, s3_ref, s1o_ref, s2o_ref, s3o_ref, s4_ref,
    out_ref, own_ref,
    xs_ref, ss_ref, sems,
):
    y, x, z, k, l = (at_ref[i] for i in range(5))
    d = 1 - 2 * k

    def copy(source, row, i):
        return pltpu.make_async_copy(source, ss_ref.at[pl.ds(lax.rem(row + 16, 8) * 256, 256)], sems.at[i])

    copies = [
        copy(s0_ref.at[k], y, 0),
        copy(s1_ref.at[k], y - d, 1),
        copy(s2_ref.at[k], y - 2 * d, 2),
        copy(s3_ref.at[k], y - 3 * d, 3),
        copy(s1o_ref.at[k], y + d, 4),
        copy(s2o_ref.at[k], y + 2 * d, 5),
        copy(s3o_ref.at[k], y + 3 * d, 6),
        copy(s4_ref, y + 4, 7),
    ]
    for c in copies:
        c.start()

    def place(slab, x_at, zsel, g):
        row = 2 * lax.rem(x_at + 8, 4) + lax.rem(z + zsel, 2)
        which = row * 2 + g
        column = pl.multiple_of(which * BLK, BLK)
        for i in range(8):
            part = slab[pl.ds(i * BLK, BLK), :]
            stored = jnp.where(mask_ref[i, which] == 1, part, jnp.zeros_like(part))
            xs_ref[pl.ds(i * BLK, BLK), pl.ds(column, BLK)] = stored

    for zsel in range(2):
        for g in range(2):
            place(x0_ref.at[g, zsel], x, zsel, g)
            place(x1_ref.at[g, zsel], x - d, zsel, g)
            place(x1o_ref.at[g, zsel], x + d, zsel, g)
        place(x2_ref.at[zsel], x + 2, zsel, k)
        place(x2o_ref.at[zsel], x + 2, zsel, 1 - k)

    for c in copies:
        c.wait()

    def region(j, carry):
        rows = pl.ds(pl.multiple_of(j * 2 * BLK, 2 * BLK), 2 * BLK)
        value = jnp.dot(xs_ref[rows, :], ss_ref[...], preferred_element_type=jnp.float32)
        flags = [keep_ref[j * 2 + a, b] == 1 for a in range(2) for b in range(4)]
        blocks = [value[a * BLK:(a + 1) * BLK, b * BLK:(b + 1) * BLK] for a in range(2) for b in range(4)]
        top = jnp.zeros((8, BLK), jnp.float32)
        for flag, block in zip(flags, blocks):
            high = jnp.max(jnp.abs(block).reshape(BLK // 8, 8, BLK), axis=0)
            top = jnp.maximum(top, jnp.where(flag, high, 0.0))
        top = jnp.max(top, axis=(0, 1), keepdims=True)
        level = jnp.ceil(8.0 * jnp.log2(jnp.maximum(top, 1e-30)))
        level = jnp.broadcast_to(level, (EXTRA, BLK))
        factor = jnp.exp2(level * -0.125) * LEVELS
        out_ref[j, pl.ds(KEPT * BLK, EXTRA), :] = level.astype(jnp.int32).astype(jnp.int16)
        at = jnp.int32(0)
        for flag, block in zip(flags, blocks):
            spot = pl.ds(pl.multiple_of(at * BLK, BLK), BLK)

            @pl.when(flag)
            def _():
                scaled = jnp.round(block * factor[0:1, :])
                out_ref[j, spot, :] = scaled.astype(jnp.int32).astype(jnp.int16)

            @pl.when(jnp.logical_and(flag, j == l))
            def _():
                own_ref[spot, :] = block

            at = at + flag.astype(jnp.int32)
        return carry

    lax.fori_loop(0, LAYERS, region, 0)


def product(at, mask, keep, xs, ss):
    smem = pl.BlockSpec(memory_space=pltpu.SMEM)
    vmem = pl.BlockSpec(memory_space=pltpu.VMEM)
    return pl.pallas_call(
        product_kernel,
        out_shape=(
            jax.ShapeDtypeStruct((LAYERS, KEPT * BLK + EXTRA, BLK), jnp.int16),
            jax.ShapeDtypeStruct((KEPT * BLK, BLK), jnp.float32),
        ),
        in_specs=[smem] * 3 + [vmem] * 5 + [pl.BlockSpec(memory_space=pl.ANY)] * 8,
        out_specs=(vmem, vmem),
        scratch_shapes=[
            pltpu.VMEM((1024, 2048), jnp.bfloat16),
            pltpu.VMEM((2048, 512), jnp.bfloat16),
            pltpu.SemaphoreType.DMA((8,)),
        ],
        compiler_params=pltpu.CompilerParams(vmem_limit_bytes=28 * 2**20),
        cost_estimate=pl.CostEstimate(flops=2 * 1024 * 2048 * 512, bytes_accessed=9 * 2**20, transcendentals=0),
    )(at, mask, keep, *xs, *ss)


def finish_kernel(at_ref, keep_ref, got_ref, own_ref, out_ref):
    l = at_ref[4]
    scales = []
    for j in range(LAYERS):
        level = got_ref[j, pl.ds(KEPT * BLK, EXTRA), :].astype(jnp.int32).astype(jnp.float32)
        scale = jnp.exp2(level * 0.125) * (1.0 / LEVELS)
        scales.append(jnp.where(j == l, 0.0, scale)[0:1, :])
    at = jnp.int32(0)
    for a in range(2):
        for b in range(4):
            flag = keep_ref[l * 2 + a, b] == 1
            spot = pl.ds(pl.multiple_of(jnp.minimum(at, KEPT - 1) * BLK, BLK), BLK)
            total = own_ref[spot, :]
            for j in range(LAYERS):
                total = total + got_ref[j, spot, :].astype(jnp.int32).astype(jnp.float32) * scales[j]
            total = jnp.where(flag, total, 0.0)
            out_ref[a * BLK:(a + 1) * BLK, b * BLK:(b + 1) * BLK] = total.astype(jnp.bfloat16)
            at = at + flag.astype(jnp.int32)


def finish(at, keep, got, own):
    smem = pl.BlockSpec(memory_space=pltpu.SMEM)
    vmem = pl.BlockSpec(memory_space=pltpu.VMEM)
    return pl.pallas_call(
        finish_kernel,
        out_shape=jax.ShapeDtypeStruct((2 * BLK, 4 * BLK), jnp.bfloat16),
        in_specs=[smem, smem, vmem, vmem],
        out_specs=vmem,
        compiler_params=pltpu.CompilerParams(vmem_limit_bytes=8 * 2**20),
        cost_estimate=pl.CostEstimate(flops=2**20, bytes_accessed=2 * 2**20, transcendentals=0),
    )(at, keep, got, own)


def shards(sign_iterate, square, pattern, keep):
    l = lax.axis_index("layer")
    y = lax.axis_index("row")
    c = lax.axis_index("col")
    k = c % 2
    at = jnp.stack([y, c // 4, (c // 2) % 2, k, l]).astype(jnp.int32)
    mask = lax.dynamic_slice(pattern, (y * 8, 0), (8, 64)).reshape(8, 16, 4)
    mask = lax.dynamic_index_in_dim(mask, l, 2, False)
    keep_here = lax.dynamic_slice(keep, (y * 8, c * 4), (8, 4))

    def half(value):
        return lax.dynamic_index_in_dim(value, k, 0, False)

    x_other = lax.dynamic_slice_in_dim(sign_iterate, (l ^ 2) * BLK, BLK, 1)
    x_z = send(x_other, ACROSS_Z)
    s_own = lax.dynamic_index_in_dim(square.reshape(2, LAYERS, BLK, 512), l, 1, False).reshape(256, 512)
    s0 = both_cores(s_own)
    s1 = send(s0, ALONG_Y)
    x_own = lax.dynamic_slice_in_dim(sign_iterate, l * BLK, BLK, 1)
    x0 = both_cores(jnp.stack([x_own, x_z]))
    x1 = send(x0, ALONG_X)
    s2 = send(s1, ALONG_Y)
    s1o = send(s1, OTHER_CORE)
    s3 = send(s2, ALONG_Y)
    s2o = send(s2, OTHER_CORE)
    x2 = send(half(x1), ALONG_X)
    s4 = send(half(s3), ALONG_Y)
    s3o = send(s3, OTHER_CORE)
    x1o = send(x1, OTHER_CORE)
    x2o = send(x2, OTHER_CORE)
    xs = (x0, x1, x1o, x2, x2o)
    sent, own = product(at, mask, keep_here, xs, (s0, s1, s2, s3, s1o, s2o, s3o, s4))
    got = lax.all_to_all(sent, "layer", 0, 0, tiled=True)
    return finish(at, keep_here, got, own)


def solution(mesh):
    return jax.shard_map(
        shards,
        mesh=mesh,
        in_specs=(P("row", "col"), P("row", "col"), P(), P()),
        out_specs=P(("row", "layer"), "col"),
        check_vma=False,
    )
```

```python
import functools

import jax
import jax.numpy as jnp
from jax import lax
from jax.experimental import pallas as pl
from jax.experimental.pallas import tpu as pltpu
from jax.sharding import PartitionSpec as P


BLK = 128
AXES = ("row", "col", "layer")
ROWS, XS, LAYERS = 8, 4, 4
KEPT = 6
EXTRA = 16
LEVELS = 32000.0


def table(move):
    pairs = []
    for r in range(ROWS):
        for x in range(XS):
            for z in range(2):
                for k in range(2):
                    for l in range(LAYERS):
                        r2, x2, z2, k2, l2 = move(r, x, z, k, l)
                        here = (r * 16 + x * 4 + z * 2 + k) * LAYERS + l
                        there = ((r2 % ROWS) * 16 + (x2 % XS) * 4 + z2 * 2 + k2) * LAYERS + l2
                        pairs.append((here, there))
    return pairs


ALONG_Y = table(lambda r, x, z, k, l: (r + 1 - 2 * k, x, z, k, l))
ALONG_X = table(lambda r, x, z, k, l: (r, x + 1 - 2 * k, z, k, l))
ACROSS_Z = table(lambda r, x, z, k, l: (r, x, 1 - z, k, l ^ 2))
OTHER_CORE = table(lambda r, x, z, k, l: (r, x, z, 1 - k, l))
CORE_PAIRS = [[2 * i, 2 * i + 1] for i in range(8)]


def both_cores(value):
    return lax.all_gather(value, "col", axis=0, tiled=False, axis_index_groups=CORE_PAIRS)


def assemble_kernel(at_ref, s0_ref, s1_ref, s2_ref, s3_ref, s1o_ref, s2o_ref, s3o_ref, s4_ref, ss_ref, sems):
    y, k = at_ref[0], at_ref[3]
    d = 1 - 2 * k
    pieces = [
        (s0_ref, y), (s1_ref, y - d), (s2_ref, y - 2 * d), (s3_ref, y - 3 * d),
        (s1o_ref, y + d), (s2o_ref, y + 2 * d), (s3o_ref, y + 3 * d), (s4_ref, y + 4),
    ]
    copies = [
        pltpu.make_async_copy(piece.at[k], ss_ref.at[lax.rem(row + 16, 8)], sems.at[i])
        for i, (piece, row) in enumerate(pieces)
    ]
    for c in copies:
        c.start()
    for c in copies:
        c.wait()


def assemble(at, pieces):
    anywhere = pl.BlockSpec(memory_space=pl.ANY)
    return pl.pallas_call(
        assemble_kernel,
        out_shape=jax.ShapeDtypeStruct((ROWS, 2 * BLK, 4 * BLK), jnp.bfloat16),
        in_specs=[pl.BlockSpec(memory_space=pltpu.SMEM)] + [anywhere] * 8,
        out_specs=pl.BlockSpec(memory_space=pltpu.VMEM),
        scratch_shapes=[pltpu.SemaphoreType.DMA((8,))],
        compiler_params=pltpu.CompilerParams(vmem_limit_bytes=6 * 2**20),
        cost_estimate=pl.CostEstimate(flops=0, bytes_accessed=4 * 2**20, transcendentals=0),
        name="assemble",
    )(at, *pieces)


def region_kernel(shift, at_ref, mask_ref, keep_ref, x0_ref, x1_ref, x1o_ref, x2_ref, ss_ref, out_ref, xs_ref):
    x, z, k, l = (at_ref[i] for i in range(1, 5))
    d = 1 - 2 * k
    j = lax.rem(l + shift, LAYERS)
    for slab, x_at in ((x0_ref, x), (x1_ref, x - d), (x1o_ref, x + d), (x2_ref, x + 2)):
        for zsel in range(2):
            row = 2 * lax.rem(x_at + 8, 4) + lax.rem(z + zsel, 2)
            for g in range(2):
                which = row * 2 + g
                column = pl.ds(pl.multiple_of(which * BLK, BLK), BLK)
                for a in range(2):
                    part = slab[zsel, g, a * BLK:(a + 1) * BLK, :]
                    stored = jnp.where(mask_ref[j * 2 + a, which] == 1, part, jnp.zeros_like(part))
                    xs_ref[a * BLK:(a + 1) * BLK, column] = stored
    value = jnp.dot(xs_ref[...], ss_ref[...].reshape(2048, 512), preferred_element_type=jnp.float32)
    flags = [keep_ref[j * 2 + a, b] == 1 for a in range(2) for b in range(4)]
    blocks = [value[a * BLK:(a + 1) * BLK, b * BLK:(b + 1) * BLK] for a in range(2) for b in range(4)]
    if shift:
        top = jnp.zeros((8, BLK), jnp.float32)
        for flag, block in zip(flags, blocks):
            high = jnp.max(jnp.abs(block).reshape(BLK // 8, 8, BLK), axis=0)
            top = jnp.maximum(top, jnp.where(flag, high, 0.0))
        top = jnp.max(top, axis=(0, 1), keepdims=True)
        level = jnp.ceil(8.0 * jnp.log2(jnp.maximum(top, 1e-30)))
        level = jnp.broadcast_to(level, (EXTRA, BLK))
        factor = (jnp.exp2(level * -0.125) * LEVELS)[0:1, :]
        out_ref[pl.ds(KEPT * BLK, EXTRA), :] = level.astype(jnp.int32).astype(jnp.int16)
        blocks = [jnp.round(block * factor).astype(jnp.int32).astype(jnp.int16) for block in blocks]
    at = jnp.int32(0)
    for flag, block in zip(flags, blocks):
        spot = pl.ds(pl.multiple_of(at * BLK, BLK), BLK)

        @pl.when(flag)
        def _():
            out_ref[spot, :] = block

        at = at + flag.astype(jnp.int32)


def region(shift, at, mask, keep, xs, ss):
    rows = pl.BlockSpec(
        (2, 2, 2 * BLK, BLK), lambda i, at, mask, keep: (0, 0, lax.rem(at[4] + shift, LAYERS), 0)
    )
    whole = pl.BlockSpec(memory_space=pltpu.VMEM)
    shape = (KEPT * BLK + EXTRA, BLK) if shift else (KEPT * BLK, BLK)
    return pl.pallas_call(
        functools.partial(region_kernel, shift),
        out_shape=jax.ShapeDtypeStruct(shape, jnp.int16 if shift else jnp.float32),
        grid_spec=pltpu.PrefetchScalarGridSpec(
            num_scalar_prefetch=3,
            grid=(1,),
            in_specs=[rows] * 4 + [whole],
            out_specs=whole,
            scratch_shapes=[pltpu.VMEM((2 * BLK, 2048), jnp.bfloat16)],
        ),
        compiler_params=pltpu.CompilerParams(vmem_limit_bytes=12 * 2**20),
        cost_estimate=pl.CostEstimate(flops=2 * 256 * 2048 * 512, bytes_accessed=4 * 2**20, transcendentals=0),
    )(at, mask, keep, *xs, ss)


def finish_kernel(at_ref, keep_ref, own_ref, *refs):
    *got_refs, out_ref = refs
    l = at_ref[4]
    scales = []
    for got in got_refs:
        level = got[pl.ds(KEPT * BLK, EXTRA), :].astype(jnp.int32).astype(jnp.float32)
        scales.append((jnp.exp2(level * 0.125) * (1.0 / LEVELS))[0:1, :])
    at = jnp.int32(0)
    for a in range(2):
        for b in range(4):
            flag = keep_ref[l * 2 + a, b] == 1
            spot = pl.ds(pl.multiple_of(jnp.minimum(at, KEPT - 1) * BLK, BLK), BLK)
            total = own_ref[spot, :]
            for got, scale in zip(got_refs, scales):
                total = total + got[spot, :].astype(jnp.int32).astype(jnp.float32) * scale
            total = jnp.where(flag, total, 0.0)
            out_ref[a * BLK:(a + 1) * BLK, b * BLK:(b + 1) * BLK] = total.astype(jnp.bfloat16)
            at = at + flag.astype(jnp.int32)


def finish(at, keep, own, got):
    smem = pl.BlockSpec(memory_space=pltpu.SMEM)
    vmem = pl.BlockSpec(memory_space=pltpu.VMEM)
    return pl.pallas_call(
        finish_kernel,
        out_shape=jax.ShapeDtypeStruct((2 * BLK, 4 * BLK), jnp.bfloat16),
        in_specs=[smem, smem] + [vmem] * 4,
        out_specs=vmem,
        compiler_params=pltpu.CompilerParams(vmem_limit_bytes=8 * 2**20),
        cost_estimate=pl.CostEstimate(flops=2**20, bytes_accessed=2 * 2**20, transcendentals=0),
        name="finish",
    )(at, keep, own, *got)


def body(sign_iterate, square, pattern, keep):
    l = lax.axis_index("layer")
    y = lax.axis_index("row")
    c = lax.axis_index("col")
    k = c % 2
    at = jnp.stack([y, c // 4, (c // 2) % 2, k, l]).astype(jnp.int32)
    mask = lax.dynamic_slice(pattern, (y * 8, 0), (8, 64)).reshape(8, 16, 4)
    mask = lax.dynamic_index_in_dim(mask, l, 2, False)
    keep_here = lax.dynamic_slice(keep, (y * 8, c * 4), (8, 4))

    def step(value, pairs):
        return lax.ppermute(value, AXES, pairs)

    x_other = lax.dynamic_slice_in_dim(sign_iterate, (l ^ 2) * BLK, BLK, 1)
    x_z = step(x_other, ACROSS_Z)
    s_own = lax.dynamic_index_in_dim(square.reshape(2, LAYERS, BLK, 512), l, 1, False).reshape(256, 512)
    s0 = both_cores(s_own)
    s1 = step(s0, ALONG_Y)
    x_own = lax.dynamic_slice_in_dim(sign_iterate, l * BLK, BLK, 1)
    x0 = jnp.stack([both_cores(x_own), both_cores(x_z)])
    x1 = step(x0, ALONG_X)
    s2 = step(s1, ALONG_Y)
    s1o = step(s1, OTHER_CORE)
    s3 = step(s2, ALONG_Y)
    s2o = step(s2, OTHER_CORE)
    x2 = step(x1, ALONG_X)
    s4 = step(s3, ALONG_Y)
    x1o = step(x1, OTHER_CORE)
    s3o = step(s3, OTHER_CORE)
    ss = assemble(at, (s0, s1, s2, s3, s1o, s2o, s3o, s4))
    xs = (x0, x1, x1o, x2)
    got = []
    for shift in (2, 1, 3):
        part = region(shift, at, mask, keep_here, xs, ss)
        pairs = table(lambda r, x, z, k, l, shift=shift: (r, x, z, k, (l + shift) % LAYERS))
        got.append(step(part, pairs))
    own = region(0, at, mask, keep_here, xs, ss)
    return finish(at, keep_here, own, got)


def solution(mesh):
    return jax.shard_map(
        body,
        mesh=mesh,
        in_specs=(P("row", "col"), P("row", "col"), P(), P()),
        out_specs=P(("row", "layer"), "col"),
        check_vma=False,
    )
```

```python
import functools

import jax
import jax.numpy as jnp
from jax import lax
from jax.experimental import pallas as pl
from jax.experimental.pallas import tpu as pltpu
from jax.sharding import PartitionSpec as P


BLK = 128
AXES = ("row", "col", "layer")
ROWS, XS, LAYERS = 8, 4, 4
KEPT = 6
EXTRA = 16
LEVELS = 32000.0


def table(move):
    pairs = []
    for r in range(ROWS):
        for x in range(XS):
            for z in range(2):
                for k in range(2):
                    for l in range(LAYERS):
                        r2, x2, z2, k2, l2 = move(r, x, z, k, l)
                        here = (r * 16 + x * 4 + z * 2 + k) * LAYERS + l
                        there = ((r2 % ROWS) * 16 + (x2 % XS) * 4 + z2 * 2 + k2) * LAYERS + l2
                        pairs.append((here, there))
    return pairs


ALONG_X = table(lambda r, x, z, k, l: (r, x + 1 - 2 * k, z, k, l))
ACROSS_Z = table(lambda r, x, z, k, l: (r, x, 1 - z, k, l ^ 2))
OTHER_CORE = table(lambda r, x, z, k, l: (r, x, z, 1 - k, l))
CORE_PAIRS = [[2 * i, 2 * i + 1] for i in range(8)]


def both_cores(value):
    return lax.all_gather(value, "col", axis=0, tiled=False, axis_index_groups=CORE_PAIRS)


def place(xs_ref, slab, row, rows, mask_ref, row_at, at):
    for g in range(2):
        column = pl.ds(pl.multiple_of(at * 2 * BLK + g * BLK, BLK), BLK)
        for i in range(rows):
            lines = pl.ds(pl.multiple_of((row_at + i) * BLK, BLK), BLK)
            part = slab[g, lines, :]
            stored = jnp.where(mask_ref[row_at + i, row * 2 + g] == 1, part, jnp.zeros_like(part))
            xs_ref[i * BLK:(i + 1) * BLK, column] = stored


def early_kernel(at_ref, mask_ref, *refs):
    slabs, refs = refs[:7], refs[7:]
    pieces, (out_ref, last_ref, xs_ref) = refs[:9], refs[9:]
    y, x, z, k = (at_ref[i] for i in range(4))
    d = 1 - 2 * k
    places = ((x, 0), (x - d, 0), (x + d, 0), (x, 1), (x - d, 1), (x + d, 1), (x + 2, 1))
    for slab, (x_at, zsel) in zip(slabs, places):
        row = 2 * lax.rem(x_at + 8, XS) + lax.rem(z + zsel, 2)
        place(xs_ref, slab, row, 8, mask_ref, 0, lax.rem(row - y + 8, ROWS))
    late = lax.rem(2 * lax.rem(x + 2, XS) + z - y + 8, ROWS)
    column = pl.ds(pl.multiple_of(late * 2 * BLK, BLK), 2 * BLK)
    xs_ref[:, column] = jnp.zeros((1024, 2 * BLK), jnp.bfloat16)
    whole = [pieces[i][...] for i in range(4)]
    whole.append(jnp.concatenate([pieces[4][...], pieces[5][...]], axis=0))
    whole += [pieces[i][...] for i in range(6, 9)]
    for i, piece in enumerate(whole):

        @pl.when(late == i)
        def _():
            last_ref[...] = piece

    def rows(i, carry):
        lines = pl.ds(pl.multiple_of(i * 2 * BLK, 2 * BLK), 2 * BLK)
        right = jnp.concatenate(whole, axis=0)
        out_ref[lines, :] = jnp.dot(xs_ref[lines, :], right, preferred_element_type=jnp.float32)
        return carry

    lax.fori_loop(0, 4, rows, 0)


SMEM = pl.BlockSpec(memory_space=pltpu.SMEM)
VMEM = pl.BlockSpec(memory_space=pltpu.VMEM)


def early(at, mask, slabs, pieces):
    return pl.pallas_call(
        early_kernel,
        out_shape=(
            jax.ShapeDtypeStruct((1024, 512), jnp.float32),
            jax.ShapeDtypeStruct((2 * BLK, 512), jnp.bfloat16),
        ),
        in_specs=[SMEM] * 2 + [VMEM] * 16,
        out_specs=(VMEM, VMEM),
        scratch_shapes=[pltpu.VMEM((1024, 2048), jnp.bfloat16)],
        compiler_params=pltpu.CompilerParams(vmem_limit_bytes=20 * 2**20),
        cost_estimate=pl.CostEstimate(flops=2 * 1024 * 2048 * 512, bytes_accessed=4 * 2**20, transcendentals=0),
        name="early",
    )(at, mask, *slabs, *pieces)


def kept(keep_ref, j):
    flags = [keep_ref[j * 2 + a, b] == 1 for a in range(2) for b in range(4)]
    spots, at = [], jnp.int32(0)
    for flag in flags:
        spots.append(pl.ds(pl.multiple_of(jnp.minimum(at, KEPT - 1) * BLK, BLK), BLK))
        at = at + flag.astype(jnp.int32)
    return flags, spots


def late_kernel(shifts, at_ref, mask_ref, keep_ref, slab_ref, last_ref, sum_ref, *refs):
    outs, xs_ref = refs[:-1], refs[-1]
    x, z, _, l = (at_ref[i] for i in range(1, 5))
    row = 2 * lax.rem(x + 2, XS) + z
    for shift, out_ref in zip(shifts, outs):
        j = lax.rem(l + shift, LAYERS)
        place(xs_ref, slab_ref, row, 2, mask_ref, j * 2, 0)
        lines = pl.ds(pl.multiple_of(j * 2 * BLK, 2 * BLK), 2 * BLK)
        value = sum_ref[lines, :] + jnp.dot(xs_ref[...], last_ref[...], preferred_element_type=jnp.float32)
        flags, spots = kept(keep_ref, j)
        blocks = [value[a * BLK:(a + 1) * BLK, b * BLK:(b + 1) * BLK] for a in range(2) for b in range(4)]
        if shift:
            top = jnp.zeros((8, BLK), jnp.float32)
            for flag, block in zip(flags, blocks):
                high = jnp.max(jnp.abs(block).reshape(BLK // 8, 8, BLK), axis=0)
                top = jnp.maximum(top, jnp.where(flag, high, 0.0))
            top = jnp.max(top, axis=(0, 1), keepdims=True)
            level = jnp.ceil(8.0 * jnp.log2(jnp.maximum(top, 1e-30)))
            level = jnp.broadcast_to(level, (EXTRA, BLK))
            factor = (jnp.exp2(level * -0.125) * LEVELS)[0:1, :]
            out_ref[pl.ds(KEPT * BLK, EXTRA), :] = level.astype(jnp.int32).astype(jnp.int16)
            blocks = [jnp.round(block * factor).astype(jnp.int32).astype(jnp.int16) for block in blocks]
        for flag, spot, block in zip(flags, spots, blocks):

            @pl.when(flag)
            def _():
                out_ref[spot, :] = block


def late(shifts, at, mask, keep, slab, last, total):
    coded = jax.ShapeDtypeStruct((KEPT * BLK + EXTRA, BLK), jnp.int16)
    plain = jax.ShapeDtypeStruct((KEPT * BLK, BLK), jnp.float32)
    return pl.pallas_call(
        functools.partial(late_kernel, shifts),
        out_shape=tuple(coded if shift else plain for shift in shifts),
        in_specs=[SMEM] * 3 + [VMEM] * 3,
        out_specs=tuple(VMEM for _ in shifts),
        scratch_shapes=[pltpu.VMEM((2 * BLK, 2 * BLK), jnp.bfloat16)],
        compiler_params=pltpu.CompilerParams(vmem_limit_bytes=12 * 2**20),
        cost_estimate=pl.CostEstimate(
            flops=len(shifts) * 2 * 256 * 256 * 512, bytes_accessed=len(shifts) * 2**20, transcendentals=0
        ),
    )(at, mask, keep, slab, last, total)


def finish_kernel(at_ref, keep_ref, own_ref, *refs):
    *got_refs, out_ref = refs
    l = at_ref[4]
    scales = []
    for got in got_refs:
        level = got[pl.ds(KEPT * BLK, EXTRA), :].astype(jnp.int32).astype(jnp.float32)
        scales.append((jnp.exp2(level * 0.125) * (1.0 / LEVELS))[0:1, :])
    at = jnp.int32(0)
    for a in range(2):
        for b in range(4):
            flag = keep_ref[l * 2 + a, b] == 1
            spot = pl.ds(pl.multiple_of(jnp.minimum(at, KEPT - 1) * BLK, BLK), BLK)
            total = own_ref[spot, :]
            for got, scale in zip(got_refs, scales):
                total = total + got[spot, :].astype(jnp.int32).astype(jnp.float32) * scale
            total = jnp.where(flag, total, 0.0)
            out_ref[a * BLK:(a + 1) * BLK, b * BLK:(b + 1) * BLK] = total.astype(jnp.bfloat16)
            at = at + flag.astype(jnp.int32)


def finish(at, keep, own, got):
    smem = pl.BlockSpec(memory_space=pltpu.SMEM)
    vmem = pl.BlockSpec(memory_space=pltpu.VMEM)
    return pl.pallas_call(
        finish_kernel,
        out_shape=jax.ShapeDtypeStruct((2 * BLK, 4 * BLK), jnp.bfloat16),
        in_specs=[smem, smem] + [vmem] * 4,
        out_specs=vmem,
        compiler_params=pltpu.CompilerParams(vmem_limit_bytes=8 * 2**20),
        cost_estimate=pl.CostEstimate(flops=2**20, bytes_accessed=2 * 2**20, transcendentals=0),
        name="finish",
    )(at, keep, own, *got)


def body(sign_iterate, square, pattern, keep):
    l = lax.axis_index("layer")
    y = lax.axis_index("row")
    c = lax.axis_index("col")
    k = c % 2
    at = jnp.stack([y, c // 4, (c // 2) % 2, k, l]).astype(jnp.int32)
    mask = lax.dynamic_slice(pattern, (y * 8, 0), (8, 64)).reshape(8, 16, 4)
    mask = lax.dynamic_index_in_dim(mask, l, 2, False)
    keep_here = lax.dynamic_slice(keep, (y * 8, c * 4), (8, 4))

    def step(value, pairs):
        return lax.ppermute(value, AXES, pairs)

    def down(value, shift):
        return step(value, table(lambda r, x, z, k, l: (r + shift, x, z, k, l)))

    z_send = lax.dynamic_slice_in_dim(sign_iterate, (l ^ 2) * BLK, BLK, 1)
    z_own = step(z_send, ACROSS_Z)
    s0 = lax.dynamic_index_in_dim(square.reshape(2, LAYERS, BLK, 512), l, 1, False).reshape(256, 512)
    s7 = down(s0, 1)
    s1 = down(s0, -1)
    s6 = down(s0, 2)
    s2 = down(s0, -2)
    z0 = both_cores(z_own)
    z1 = step(z0, ALONG_X)
    x0 = both_cores(lax.dynamic_slice_in_dim(sign_iterate, l * BLK, BLK, 1))
    x1 = step(x0, ALONG_X)
    s4a = down(s6[:BLK], 2)
    s4b = down(s2[BLK:], -2)
    z2 = step(z1, ALONG_X)
    s5 = down(s6, 1)
    s3 = down(s2, -1)
    x2 = step(x1, ALONG_X)
    x1o = step(x1, OTHER_CORE)
    z1o = step(z1, OTHER_CORE)
    total, last = early(at, mask, (x0, x1, x1o, z0, z1, z1o, z2), (s0, s1, s2, s3, s4a, s4b, s5, s6, s7))
    shifts = (2, 1, 3)
    parts = late(shifts, at, mask, keep_here, x2, last, total)
    got = []
    for shift, part in zip(shifts, parts):
        pairs = table(lambda r, x, z, k, l: (r, x, z, k, (l + shift) % LAYERS))
        got.append(step(part, pairs))
    (own,) = late((0,), at, mask, keep_here, x2, last, total)
    return finish(at, keep_here, own, got)


def solution(mesh):
    return jax.shard_map(
        body,
        mesh=mesh,
        in_specs=(P("row", "col"), P("row", "col"), P(), P()),
        out_specs=P(("row", "layer"), "col"),
        check_vma=False,
    )
```

```python
import functools

import jax
import jax.numpy as jnp
from jax import lax
from jax.experimental import pallas as pl
from jax.experimental.pallas import tpu as pltpu
from jax.sharding import PartitionSpec as P


BLK = 128
AXES = ("row", "col", "layer")
ROWS, XS, LAYERS = 8, 4, 4
KEPT = 6
EXTRA = 16
LEVELS = 32000.0


def table(move):
    pairs = []
    for r in range(ROWS):
        for x in range(XS):
            for z in range(2):
                for k in range(2):
                    for l in range(LAYERS):
                        r2, x2, z2, k2, l2 = move(r, x, z, k, l)
                        here = (r * 16 + x * 4 + z * 2 + k) * LAYERS + l
                        there = ((r2 % ROWS) * 16 + (x2 % XS) * 4 + z2 * 2 + k2) * LAYERS + l2
                        pairs.append((here, there))
    return pairs


ALONG_X = table(lambda r, x, z, k, l: (r, x + 1 - 2 * k, z, k, l))
ACROSS_Z = table(lambda r, x, z, k, l: (r, x, 1 - z, k, l ^ 2))
OTHER_CORE = table(lambda r, x, z, k, l: (r, x, z, 1 - k, l))
CORE_PAIRS = [[2 * i, 2 * i + 1] for i in range(8)]


def both_cores(value):
    return lax.all_gather(value, "col", axis=0, tiled=False, axis_index_groups=CORE_PAIRS)


def place(xs_ref, slab, row, at, pattern_ref, y, l):
    for g in range(2):
        column = pl.ds(pl.multiple_of(at * 2 * BLK + g * BLK, BLK), BLK)
        for i in range(8):
            part = slab[g, i * BLK:(i + 1) * BLK, :]
            stored = pattern_ref[y * 8 + i, (row * 2 + g) * LAYERS + l] == 1
            xs_ref[i * BLK:(i + 1) * BLK, column] = jnp.where(stored, part, jnp.zeros_like(part))


def early_kernel(at_ref, pattern_ref, *refs):
    slabs, refs = refs[:8], refs[8:]
    (s0_ref, d1_ref, d2_ref, d3_ref, s4_ref), (out_ref, xs_ref) = refs[:5], refs[5:]
    y, x, z, k, l = (at_ref[i] for i in range(5))
    d = 1 - 2 * k
    places = [(x_at, zsel) for zsel in range(2) for x_at in (x, x - d, x + d, x + 2)]
    for slab, (x_at, zsel) in zip(slabs, places):
        row = 2 * lax.rem(x_at + 8, XS) + lax.rem(z + zsel, 2)
        step = lax.rem(d * (y - row) + 16, ROWS)
        at = jnp.where(step <= 4, step, 12 - step)
        place(xs_ref, slab, row, at, pattern_ref, y, l)

    def rows(i, carry):
        lines = pl.ds(pl.multiple_of(i * 2 * BLK, 2 * BLK), 2 * BLK)
        right = jnp.concatenate([s0_ref[...], d1_ref[k], d2_ref[k], d3_ref[k], s4_ref[...]], axis=0)
        out_ref[lines, :] = jnp.dot(xs_ref[lines, :5 * 2 * BLK], right, preferred_element_type=jnp.float32)
        return carry

    lax.fori_loop(0, 4, rows, 0)


SMEM = pl.BlockSpec(memory_space=pltpu.SMEM)
VMEM = pl.BlockSpec(memory_space=pltpu.VMEM)


def early(at, pattern, slabs, pieces):
    return pl.pallas_call(
        early_kernel,
        out_shape=(
            jax.ShapeDtypeStruct((1024, 512), jnp.float32),
            jax.ShapeDtypeStruct((1024, 2048), jnp.bfloat16),
        ),
        in_specs=[SMEM] * 2 + [VMEM] * 13,
        out_specs=(VMEM, VMEM),
        compiler_params=pltpu.CompilerParams(vmem_limit_bytes=13 * 2**20),
        cost_estimate=pl.CostEstimate(flops=2 * 1024 * 1280 * 512, bytes_accessed=4 * 2**20, transcendentals=0),
        name="early",
    )(at, pattern, *slabs, *pieces)


def kept(keep_ref, at_ref, j):
    y, c = at_ref[0], at_ref[5]
    flags = [keep_ref[y * 8 + j * 2 + a, c * 4 + b] == 1 for a in range(2) for b in range(4)]
    spots, at = [], jnp.int32(0)
    for flag in flags:
        spots.append(pl.ds(pl.multiple_of(jnp.minimum(at, KEPT - 1) * BLK, BLK), BLK))
        at = at + flag.astype(jnp.int32)
    return flags, spots


def late_kernel(shifts, at_ref, keep_ref, swapped_ref, sum_ref, xs_ref, *outs):
    l = at_ref[4]
    for shift, out_ref in zip(shifts, outs):
        j = lax.rem(l + shift, LAYERS)
        lines = pl.ds(pl.multiple_of(j * 2 * BLK, 2 * BLK), 2 * BLK)
        right = swapped_ref[...].reshape(6 * BLK, 512)
        value = sum_ref[lines, :] + jnp.dot(xs_ref[lines, 10 * BLK:], right, preferred_element_type=jnp.float32)
        flags, spots = kept(keep_ref, at_ref, j)
        blocks = [value[a * BLK:(a + 1) * BLK, b * BLK:(b + 1) * BLK] for a in range(2) for b in range(4)]
        if shift:
            top = jnp.zeros((8, BLK), jnp.float32)
            for flag, block in zip(flags, blocks):
                high = jnp.max(jnp.abs(block).reshape(BLK // 8, 8, BLK), axis=0)
                top = jnp.maximum(top, jnp.where(flag, high, 0.0))
            top = jnp.max(top, axis=(0, 1), keepdims=True)
            level = jnp.ceil(8.0 * jnp.log2(jnp.maximum(top, 1e-30)))
            level = jnp.broadcast_to(level, (EXTRA, BLK))
            factor = (jnp.exp2(level * -0.125) * LEVELS)[0:1, :]
            out_ref[pl.ds(KEPT * BLK, EXTRA), :] = level.astype(jnp.int32).astype(jnp.int16)
            blocks = [jnp.round(block * factor).astype(jnp.int32).astype(jnp.int16) for block in blocks]
        for flag, spot, block in zip(flags, spots, blocks):

            @pl.when(flag)
            def _():
                out_ref[spot, :] = block


def late(shifts, at, keep, swapped, total, xs):
    coded = jax.ShapeDtypeStruct((KEPT * BLK + EXTRA, BLK), jnp.int16)
    plain = jax.ShapeDtypeStruct((KEPT * BLK, BLK), jnp.float32)
    return pl.pallas_call(
        functools.partial(late_kernel, shifts),
        out_shape=tuple(coded if shift else plain for shift in shifts),
        in_specs=[SMEM] * 2 + [VMEM] * 3,
        out_specs=tuple(VMEM for _ in shifts),
        compiler_params=pltpu.CompilerParams(vmem_limit_bytes=12 * 2**20),
        cost_estimate=pl.CostEstimate(
            flops=len(shifts) * 2 * 256 * 768 * 512, bytes_accessed=len(shifts) * 2**20, transcendentals=0
        ),
    )(at, keep, swapped, total, xs)


def finish_kernel(at_ref, keep_ref, own_ref, *refs):
    *got_refs, out_ref = refs
    l = at_ref[4]
    scales = []
    for got in got_refs:
        level = got[pl.ds(KEPT * BLK, EXTRA), :].astype(jnp.int32).astype(jnp.float32)
        scales.append((jnp.exp2(level * 0.125) * (1.0 / LEVELS))[0:1, :])
    flags, spots = kept(keep_ref, at_ref, l)
    for a in range(2):
        for b in range(4):
            flag, spot = flags[a * 4 + b], spots[a * 4 + b]
            total = own_ref[spot, :]
            for got, scale in zip(got_refs, scales):
                total = total + got[spot, :].astype(jnp.int32).astype(jnp.float32) * scale
            total = jnp.where(flag, total, 0.0)
            out_ref[a * BLK:(a + 1) * BLK, b * BLK:(b + 1) * BLK] = total.astype(jnp.bfloat16)


def finish(at, keep, own, got):
    smem = pl.BlockSpec(memory_space=pltpu.SMEM)
    vmem = pl.BlockSpec(memory_space=pltpu.VMEM)
    return pl.pallas_call(
        finish_kernel,
        out_shape=jax.ShapeDtypeStruct((2 * BLK, 4 * BLK), jnp.bfloat16),
        in_specs=[smem, smem] + [vmem] * 4,
        out_specs=vmem,
        compiler_params=pltpu.CompilerParams(vmem_limit_bytes=8 * 2**20),
        cost_estimate=pl.CostEstimate(flops=2**20, bytes_accessed=2 * 2**20, transcendentals=0),
        name="finish",
    )(at, keep, own, *got)


def body(sign_iterate, square, pattern, keep):
    l = lax.axis_index("layer")
    y = lax.axis_index("row")
    c = lax.axis_index("col")
    k = c % 2
    at = jnp.stack([y, c // 4, (c // 2) % 2, k, l, c]).astype(jnp.int32)

    def step(value, pairs):
        return lax.ppermute(value, AXES, pairs)

    def along(value, far):
        return step(value, table(lambda r, x, z, k, l: (r + far * (1 - 2 * k), x, z, k, l)))

    z_send = lax.dynamic_slice_in_dim(sign_iterate, (l ^ 2) * BLK, BLK, 1)
    z_own = step(z_send, ACROSS_Z)
    s0 = lax.dynamic_index_in_dim(square.reshape(2, LAYERS, BLK, 512), l, 1, False).reshape(256, 512)
    s_both = both_cores(s0)
    d1 = along(s_both, 1)
    x0 = both_cores(lax.dynamic_slice_in_dim(sign_iterate, l * BLK, BLK, 1))
    x1 = step(x0, ALONG_X)
    z0 = both_cores(z_own)
    z1 = step(z0, ALONG_X)
    d2 = along(s_both, 2)
    d3 = along(d1, 2)
    x2 = step(x1, ALONG_X)
    s4 = along(s0, 4)
    z2 = step(z1, ALONG_X)
    x1o = step(x1, OTHER_CORE)
    z1o = step(z1, OTHER_CORE)
    swapped = jnp.stack([lax.dynamic_index_in_dim(v, 1 - k, 0, False) for v in (d1, d2, d3)])
    swapped = step(swapped, OTHER_CORE)
    total, xs = early(at, pattern, (x0, x1, x1o, x2, z0, z1, z1o, z2), (s0, d1, d2, d3, s4))
    shifts = (2, 1, 3)
    parts = late(shifts, at, keep, swapped, total, xs)
    got = []
    for shift, part in zip(shifts, parts):
        pairs = table(lambda r, x, z, k, l: (r, x, z, k, (l + shift) % LAYERS))
        got.append(step(part, pairs))
    (own,) = late((0,), at, keep, swapped, total, xs)
    return finish(at, keep, own, got)


def solution(mesh):
    return jax.shard_map(
        body,
        mesh=mesh,
        in_specs=(P("row", "col"), P("row", "col"), P(), P()),
        out_specs=P(("row", "layer"), "col"),
        check_vma=False,
    )
```

```python
import functools

import jax
import jax.numpy as jnp
from jax import lax
from jax.experimental import pallas as pl
from jax.experimental.pallas import tpu as pltpu
from jax.sharding import PartitionSpec as P


BLK = 128
AXES = ("row", "col", "layer")
ROWS, XS, LAYERS = 8, 4, 4
KEPT = 6


def table(move):
    pairs = []
    for r in range(ROWS):
        for x in range(XS):
            for z in range(2):
                for k in range(2):
                    for l in range(LAYERS):
                        r2, x2, z2, k2, l2 = move(r, x, z, k, l)
                        here = (r * 16 + x * 4 + z * 2 + k) * LAYERS + l
                        there = ((r2 % ROWS) * 16 + (x2 % XS) * 4 + z2 * 2 + k2) * LAYERS + l2
                        pairs.append((here, there))
    return pairs


ALONG_X = table(lambda r, x, z, k, l: (r, x + 1 - 2 * k, z, k, l))
ACROSS_Z = table(lambda r, x, z, k, l: (r, x, 1 - z, k, l ^ 2))
OTHER_CORE = table(lambda r, x, z, k, l: (r, x, z, 1 - k, l))
CORE_PAIRS = [[2 * i, 2 * i + 1] for i in range(8)]


def both_cores(value):
    return lax.all_gather(value, "col", axis=0, tiled=False, axis_index_groups=CORE_PAIRS)


SMEM = pl.BlockSpec(memory_space=pltpu.SMEM)
VMEM = pl.BlockSpec(memory_space=pltpu.VMEM)


def place(xs_ref, column, slab, row, first, lines, pattern_ref, at_ref):
    y, l = at_ref[0], at_ref[4]
    for g in range(2):
        for b in range(2):
            spot = pl.ds(pl.multiple_of(column + g * 2 * BLK + b * BLK, BLK), BLK)
            which = row * 8 + g * 4 + lax.rem(l, 2) * 2 + b
            for i in range(lines):
                source = pl.ds(pl.multiple_of((first + i) * BLK, BLK), BLK)
                part = slab[g, source, b * BLK:(b + 1) * BLK]
                stored = pattern_ref[y * 8 + lax.div(l, 2) * 4 + first + i, which] == 1
                xs_ref[i * BLK:(i + 1) * BLK, spot] = jnp.where(stored, part, jnp.zeros_like(part))


def opposite(at_ref, zsel):
    row = 2 * lax.rem(at_ref[1] + 2, XS) + lax.rem(at_ref[2] + zsel, 2)
    return row, lax.rem(row - at_ref[0] + 8, ROWS)


def early_kernel(at_ref, pattern_ref, *refs):
    slabs, pieces, (out_ref, last_ref, xs4_ref, xs_ref, x_ref, s_ref, sems) = refs[:3], refs[3:10], refs[10:]
    y, x, z, k = (at_ref[i] for i in range(4))
    d = 1 - 2 * k
    copies = [pltpu.make_async_copy(slab, x_ref.at[i], sems.at[i]) for i, slab in enumerate(slabs)]
    copies += [pltpu.make_async_copy(piece, s_ref.at[i], sems.at[3 + i]) for i, piece in enumerate(pieces)]
    for copy in copies:
        copy.start()

    def position(step):
        return jnp.where(step < 4, step, jnp.where(step == 4, 7, step - 1))

    for i, x_at in enumerate((x, x - d, x + d)):
        copies[i].wait()
        for zsel in range(2):
            row = 2 * lax.rem(x_at + 8, XS) + lax.rem(z + zsel, 2)
            column = position(lax.rem(row - y + 8, ROWS)) * 4 * BLK
            place(xs_ref, column, x_ref.at[i, zsel], row, 0, 4, pattern_ref, at_ref)
    for copy in copies[3:]:
        copy.wait()
    for zsel in range(2):
        at = position(opposite(at_ref, zsel)[1])
        xs_ref[:, pl.ds(pl.multiple_of(at * 4 * BLK, BLK), 4 * BLK)] = jnp.zeros((512, 4 * BLK), jnp.bfloat16)
        last_ref[zsel] = s_ref[jnp.minimum(at, 6)]
    xs4_ref[...] = xs_ref[:, 28 * BLK:]
    for i in range(2):
        lines = slice(i * 2 * BLK, (i + 1) * 2 * BLK)
        right = s_ref[...].reshape(28 * BLK, 512)
        out_ref[lines, :] = jnp.dot(xs_ref[lines, :28 * BLK], right, preferred_element_type=jnp.float32)


def early(at, pattern, slabs, pieces):
    return pl.pallas_call(
        early_kernel,
        out_shape=(
            jax.ShapeDtypeStruct((512, 512), jnp.float32),
            jax.ShapeDtypeStruct((2, 512, 512), jnp.bfloat16),
            jax.ShapeDtypeStruct((512, 512), jnp.bfloat16),
        ),
        in_specs=[SMEM] * 2 + [pl.BlockSpec(memory_space=pltpu.HBM)] * 10,
        out_specs=(VMEM,) * 3,
        scratch_shapes=[
            pltpu.VMEM((512, 4096), jnp.bfloat16),
            pltpu.VMEM((3, 2, 2, 512, 256), jnp.bfloat16),
            pltpu.VMEM((7, 512, 512), jnp.bfloat16),
            pltpu.SemaphoreType.DMA((10,)),
        ],
        compiler_params=pltpu.CompilerParams(vmem_limit_bytes=16 * 2**20),
        cost_estimate=pl.CostEstimate(flops=2 * 512 * 4096 * 512, bytes_accessed=4 * 2**20, transcendentals=0),
        name="early",
    )(at, pattern, *slabs, *pieces)


def kept(keep_ref, at_ref, region):
    y, c = at_ref[0], at_ref[5]
    flags = [keep_ref[y * 8 + region * 2 + a, c * 4 + b] == 1 for a in range(2) for b in range(4)]
    spots, at = [], jnp.int32(0)
    for flag in flags:
        spots.append(pl.ds(pl.multiple_of(jnp.minimum(at, KEPT - 1) * BLK, BLK), BLK))
        at = at + flag.astype(jnp.int32)
    return flags, spots


def late_kernel(shift, at_ref, pattern_ref, keep_ref, x2_ref, s4a_ref, s4b_ref, last_ref, xs4_ref, sum_ref, out_ref, xs_ref):
    l = at_ref[4]
    part = lax.rem(l + shift, 2)
    lines = pl.ds(pl.multiple_of(part * 2 * BLK, 2 * BLK), 2 * BLK)
    xs_ref[:, :8 * BLK] = jnp.zeros((2 * BLK, 8 * BLK), jnp.bfloat16)
    xs_ref[:, 8 * BLK:] = xs4_ref[lines, :]
    for zsel in range(2):
        row, step = opposite(at_ref, zsel)
        column = jnp.where(step == 4, 2, zsel) * 4 * BLK
        place(xs_ref, column, x2_ref.at[zsel], row, part * 2, 2, pattern_ref, at_ref)
    right = jnp.concatenate([last_ref[0], last_ref[1], s4a_ref[...], s4b_ref[...]], axis=0)
    value = sum_ref[lines, :] + jnp.dot(xs_ref[...], right, preferred_element_type=jnp.float32)
    flags, spots = kept(keep_ref, at_ref, lax.div(l, 2) * 2 + part)
    for i, (flag, spot) in enumerate(zip(flags, spots)):
        a, b = i // 4, i % 4

        @pl.when(flag)
        def _():
            out_ref[spot, :] = value[a * BLK:(a + 1) * BLK, b * BLK:(b + 1) * BLK]


def late(shift, at, pattern, keep, *arrays):
    return pl.pallas_call(
        functools.partial(late_kernel, shift),
        out_shape=jax.ShapeDtypeStruct((KEPT * BLK, BLK), jnp.float32),
        in_specs=[SMEM] * 3 + [VMEM] * 6,
        out_specs=VMEM,
        scratch_shapes=[pltpu.VMEM((2 * BLK, 12 * BLK), jnp.bfloat16)],
        compiler_params=pltpu.CompilerParams(vmem_limit_bytes=12 * 2**20),
        cost_estimate=pl.CostEstimate(flops=2 * 256 * 1536 * 512, bytes_accessed=2**20, transcendentals=0),
    )(at, pattern, keep, *arrays)


def finish_kernel(at_ref, keep_ref, own_ref, got_ref, out_ref):
    flags, spots = kept(keep_ref, at_ref, at_ref[4])
    for i, (flag, spot) in enumerate(zip(flags, spots)):
        a, b = i // 4, i % 4
        total = jnp.where(flag, own_ref[spot, :] + got_ref[spot, :], 0.0)
        out_ref[a * BLK:(a + 1) * BLK, b * BLK:(b + 1) * BLK] = total.astype(jnp.bfloat16)


def finish(at, keep, own, got):
    return pl.pallas_call(
        finish_kernel,
        out_shape=jax.ShapeDtypeStruct((2 * BLK, 4 * BLK), jnp.bfloat16),
        in_specs=[SMEM, SMEM, VMEM, VMEM],
        out_specs=VMEM,
        compiler_params=pltpu.CompilerParams(vmem_limit_bytes=8 * 2**20),
        cost_estimate=pl.CostEstimate(flops=2**20, bytes_accessed=2 * 2**20, transcendentals=0),
        name="finish",
    )(at, keep, own, got)


def body(sign_iterate, square, pattern, keep):
    l = lax.axis_index("layer")
    y = lax.axis_index("row")
    c = lax.axis_index("col")
    half, part = l // 2, l % 2
    at = jnp.stack([y, c // 4, (c // 2) % 2, c % 2, l, c]).astype(jnp.int32)
    at, sign_iterate, square = lax.optimization_barrier((at, sign_iterate, square))

    def step(value, pairs):
        return lax.ppermute(value, AXES, pairs)

    def down(value, shift):
        return step(value, table(lambda r, x, z, k, l: (r + shift, x, z, k, l)))

    def slab(rows):
        return lax.dynamic_slice(sign_iterate, (rows * 512, part * 256), (512, 256))

    z_own = step(slab(1 - half), ACROSS_Z)
    s0 = lax.dynamic_index_in_dim(square.reshape(2, 2, 256, 512), part, 1, False).reshape(512, 512)
    s7 = down(s0, 1)
    s1 = down(s0, -1)
    x0 = jnp.stack([both_cores(slab(half)), both_cores(z_own)])
    x1 = step(x0, ALONG_X)
    s6 = down(s7, 1)
    s2 = down(s1, -1)
    s5 = down(s6, 1)
    s3 = down(s2, -1)
    x2 = step(x1, ALONG_X)
    x1o = step(x1, OTHER_CORE)
    s4a = down(s5[:256], 1)
    s4b = down(s3[256:], -1)
    total, last, xs4 = early(at, pattern, (x0, x1, x1o), (s0, s1, s2, s3, s5, s6, s7))
    rest = (x2, s4a, s4b, last, xs4, total)
    sent = late(1, at, pattern, keep, *rest)
    got = step(sent, table(lambda r, x, z, k, l: (r, x, z, k, l ^ 1)))
    own = late(0, at, pattern, keep, *rest)
    return finish(at, keep, own, got)


def solution(mesh):
    return jax.shard_map(
        body,
        mesh=mesh,
        in_specs=(P("row", "col"), P("row", "col"), P(), P()),
        out_specs=P(("row", "layer"), "col"),
        check_vma=False,
    )
```

```python
import functools

import jax
import jax.numpy as jnp
from jax import lax
from jax.experimental import pallas as pl
from jax.experimental.pallas import tpu as pltpu
from jax.sharding import PartitionSpec as P


BLK = 128
AXES = ("row", "col", "layer")
ROWS, XS, LAYERS = 8, 4, 4
KEPT = 6


def table(move):
    pairs = []
    for r in range(ROWS):
        for x in range(XS):
            for z in range(2):
                for k in range(2):
                    for l in range(LAYERS):
                        r2, x2, z2, k2, l2 = move(r, x, z, k, l)
                        here = (r * 16 + x * 4 + z * 2 + k) * LAYERS + l
                        there = ((r2 % ROWS) * 16 + (x2 % XS) * 4 + z2 * 2 + k2) * LAYERS + l2
                        pairs.append((here, there))
    return pairs


ALONG_X = table(lambda r, x, z, k, l: (r, x + 1 - 2 * k, z, k, l))
ACROSS_Z = table(lambda r, x, z, k, l: (r, x, 1 - z, k, l ^ 2))
OTHER_CORE = table(lambda r, x, z, k, l: (r, x, z, 1 - k, l))
CORE_PAIRS = [[2 * i, 2 * i + 1] for i in range(8)]


def both_cores(value):
    return lax.all_gather(value, "col", axis=0, tiled=False, axis_index_groups=CORE_PAIRS)


SMEM = pl.BlockSpec(memory_space=pltpu.SMEM)
VMEM = pl.BlockSpec(memory_space=pltpu.VMEM)


def place(xs_ref, column, slab, row, lines, pattern_ref, at_ref):
    y, l = at_ref[0], at_ref[4]
    for g in range(2):
        for b in range(2):
            spot = pl.ds(pl.multiple_of(column + g * 2 * BLK + b * BLK, BLK), BLK)
            which = row * 8 + g * 4 + lax.rem(l, 2) * 2 + b
            for i in range(lines):
                part = slab[g, i * BLK:(i + 1) * BLK, b * BLK:(b + 1) * BLK]
                stored = pattern_ref[y * 8 + lax.div(l, 2) * 4 + i, which] == 1
                xs_ref[i * BLK:(i + 1) * BLK, spot] = jnp.where(stored, part, jnp.zeros_like(part))


def early_kernel(at_ref, pattern_ref, *refs):
    slabs, pieces, (out_ref, xs4_ref, xs_ref) = refs[:8], refs[8:15], refs[15:]
    y, x, z, k = (at_ref[i] for i in range(4))
    d = 1 - 2 * k
    places = [(x_at, zsel) for zsel in range(2) for x_at in (x, x - d, x + d, x + 2)]
    for slab, (x_at, zsel) in zip(slabs, places):
        row = 2 * lax.rem(x_at + 8, XS) + lax.rem(z + zsel, 2)
        step = lax.rem(row - y + 8, ROWS)
        column = jnp.where(step < 4, step, jnp.where(step == 4, 7, step - 1)) * 4 * BLK
        place(xs_ref, column, slab, row, 4, pattern_ref, at_ref)
    xs4_ref[...] = xs_ref[:, 28 * BLK:]
    for i in range(2):
        lines = slice(i * 2 * BLK, (i + 1) * 2 * BLK)
        right = jnp.concatenate([piece[...] for piece in pieces], axis=0)
        out_ref[lines, :] = jnp.dot(xs_ref[lines, :28 * BLK], right, preferred_element_type=jnp.float32)


def early(at, pattern, slabs, pieces):
    return pl.pallas_call(
        early_kernel,
        out_shape=(
            jax.ShapeDtypeStruct((512, 512), jnp.float32),
            jax.ShapeDtypeStruct((512, 512), jnp.bfloat16),
        ),
        in_specs=[SMEM] * 2 + [VMEM] * 15,
        out_specs=(VMEM,) * 2,
        scratch_shapes=[pltpu.VMEM((512, 4096), jnp.bfloat16)],
        compiler_params=pltpu.CompilerParams(vmem_limit_bytes=16 * 2**20),
        cost_estimate=pl.CostEstimate(flops=2 * 512 * 3584 * 512, bytes_accessed=4 * 2**20, transcendentals=0),
        name="early",
    )(at, pattern, *slabs, *pieces)


def kept(keep_ref, at_ref, region):
    y, c = at_ref[0], at_ref[5]
    flags = [keep_ref[y * 8 + region * 2 + a, c * 4 + b] == 1 for a in range(2) for b in range(4)]
    spots, at = [], jnp.int32(0)
    for flag in flags:
        spots.append(pl.ds(pl.multiple_of(jnp.minimum(at, KEPT - 1) * BLK, BLK), BLK))
        at = at + flag.astype(jnp.int32)
    return flags, spots


def late_kernel(shift, at_ref, keep_ref, s4_ref, xs4_ref, sum_ref, out_ref):
    l = at_ref[4]
    part = lax.rem(l + shift, 2)
    lines = pl.ds(pl.multiple_of(part * 2 * BLK, 2 * BLK), 2 * BLK)
    value = sum_ref[lines, :] + jnp.dot(xs4_ref[lines, :], s4_ref[...], preferred_element_type=jnp.float32)
    flags, spots = kept(keep_ref, at_ref, lax.div(l, 2) * 2 + part)
    for i, (flag, spot) in enumerate(zip(flags, spots)):
        a, b = i // 4, i % 4

        @pl.when(flag)
        def _():
            out_ref[spot, :] = value[a * BLK:(a + 1) * BLK, b * BLK:(b + 1) * BLK]


def late(shift, at, keep, *arrays):
    return pl.pallas_call(
        functools.partial(late_kernel, shift),
        out_shape=jax.ShapeDtypeStruct((KEPT * BLK, BLK), jnp.float32),
        in_specs=[SMEM] * 2 + [VMEM] * 3,
        out_specs=VMEM,
        compiler_params=pltpu.CompilerParams(vmem_limit_bytes=8 * 2**20),
        cost_estimate=pl.CostEstimate(flops=2 * 256 * 512 * 512, bytes_accessed=2**20, transcendentals=0),
    )(at, keep, *arrays)


def finish_kernel(at_ref, keep_ref, own_ref, got_ref, out_ref):
    flags, spots = kept(keep_ref, at_ref, at_ref[4])
    for i, (flag, spot) in enumerate(zip(flags, spots)):
        a, b = i // 4, i % 4
        total = jnp.where(flag, own_ref[spot, :] + got_ref[spot, :], 0.0)
        out_ref[a * BLK:(a + 1) * BLK, b * BLK:(b + 1) * BLK] = total.astype(jnp.bfloat16)


def finish(at, keep, own, got):
    return pl.pallas_call(
        finish_kernel,
        out_shape=jax.ShapeDtypeStruct((2 * BLK, 4 * BLK), jnp.bfloat16),
        in_specs=[SMEM, SMEM, VMEM, VMEM],
        out_specs=VMEM,
        compiler_params=pltpu.CompilerParams(vmem_limit_bytes=8 * 2**20),
        cost_estimate=pl.CostEstimate(flops=2**20, bytes_accessed=2 * 2**20, transcendentals=0),
        name="finish",
    )(at, keep, own, got)


def body(sign_iterate, square, pattern, keep):
    l = lax.axis_index("layer")
    y = lax.axis_index("row")
    c = lax.axis_index("col")
    half, part = l // 2, l % 2
    at = jnp.stack([y, c // 4, (c // 2) % 2, c % 2, l, c]).astype(jnp.int32)
    at, sign_iterate, square = lax.optimization_barrier((at, sign_iterate, square))

    def step(value, pairs):
        return lax.ppermute(value, AXES, pairs)

    def down(value, shift):
        return step(value, table(lambda r, x, z, k, l: (r + shift, x, z, k, l)))

    def slab(rows):
        return lax.dynamic_slice(sign_iterate, (rows * 512, part * 256), (512, 256))

    s0 = lax.dynamic_index_in_dim(square.reshape(2, 2, 256, 512), part, 1, False).reshape(512, 512)
    s7 = down(s0, 1)
    z_own = step(slab(1 - half), ACROSS_Z)
    s1 = down(s0, -1)
    x0 = both_cores(slab(half))
    x1 = step(x0, ALONG_X)
    s6 = down(s7, 1)
    z0 = both_cores(z_own)
    z1 = step(z0, ALONG_X)
    s2 = down(s1, -1)
    s5 = down(s6, 1)
    x2 = step(x1, ALONG_X)
    z2 = step(z1, ALONG_X)
    s3 = down(s2, -1)
    s4 = down(s5, 1)
    x1o = step(x1, OTHER_CORE)
    z1o = step(z1, OTHER_CORE)
    total, xs4 = early(at, pattern, (x0, x1, x1o, x2, z0, z1, z1o, z2), (s0, s1, s2, s3, s5, s6, s7))
    sent = late(1, at, keep, s4, xs4, total)
    got = step(sent, table(lambda r, x, z, k, l: (r, x, z, k, l ^ 1)))
    own = late(0, at, keep, s4, xs4, total)
    return finish(at, keep, own, got)


def solution(mesh):
    return jax.shard_map(
        body,
        mesh=mesh,
        in_specs=(P("row", "col"), P("row", "col"), P(), P()),
        out_specs=P(("row", "layer"), "col"),
        check_vma=False,
    )
```

```python
import functools

import jax
import jax.numpy as jnp
from jax import lax
from jax.experimental import pallas as pl
from jax.experimental.pallas import tpu as pltpu
from jax.sharding import PartitionSpec as P


BLK = 128
AXES = ("row", "col", "layer")
ROWS, XS, LAYERS = 8, 4, 4
KEPT = 6


def table(move):
    pairs = []
    for r in range(ROWS):
        for x in range(XS):
            for z in range(2):
                for k in range(2):
                    for l in range(LAYERS):
                        r2, x2, z2, k2, l2 = move(r, x, z, k, l)
                        here = (r * 16 + x * 4 + z * 2 + k) * LAYERS + l
                        there = ((r2 % ROWS) * 16 + (x2 % XS) * 4 + z2 * 2 + k2) * LAYERS + l2
                        pairs.append((here, there))
    return pairs


ALONG_X = table(lambda r, x, z, k, l: (r, x + 1 - 2 * k, z, k, l))
ACROSS_Z = table(lambda r, x, z, k, l: (r, x, 1 - z, k, l ^ 2))
OTHER_CORE = table(lambda r, x, z, k, l: (r, x, z, 1 - k, l))
CORE_PAIRS = [[2 * i, 2 * i + 1] for i in range(8)]


def both_cores(value):
    return lax.all_gather(value, "col", axis=0, tiled=False, axis_index_groups=CORE_PAIRS)


SMEM = pl.BlockSpec(memory_space=pltpu.SMEM)
VMEM = pl.BlockSpec(memory_space=pltpu.VMEM)


def place(xs_ref, column, slab, row, lines, pattern_ref, at_ref):
    y, l = at_ref[0], at_ref[4]
    for g in range(2):
        for b in range(2):
            spot = pl.ds(pl.multiple_of(column + g * 2 * BLK + b * BLK, BLK), BLK)
            which = row * 8 + g * 4 + lax.rem(l, 2) * 2 + b
            for i in range(lines):
                part = slab[g, i * BLK:(i + 1) * BLK, b * BLK:(b + 1) * BLK]
                stored = pattern_ref[y * 8 + lax.div(l, 2) * 4 + i, which] == 1
                xs_ref[i * BLK:(i + 1) * BLK, spot] = jnp.where(stored, part, jnp.zeros_like(part))


def early_kernel(at_ref, pattern_ref, keep_ref, *refs):
    slabs, pieces, (out_ref, rest_ref, spots_ref, xs_ref) = refs[:8], refs[8:14], refs[14:]
    y, l, c = at_ref[0], at_ref[4], at_ref[5]
    for part in range(2):
        at = jnp.int32(0)
        for i in range(8):
            flag = keep_ref[y * 8 + (lax.div(l, 2) * 2 + part) * 2 + i // 4, c * 4 + i % 4] == 1
            spots_ref[part * 8 + i] = jnp.where(flag, jnp.minimum(at, KEPT - 1), -1)
            at = at + flag.astype(jnp.int32)
    spots_ref[16] = lax.rem(l, 2)
    y, x, z, k = (at_ref[i] for i in range(4))
    d = 1 - 2 * k
    places = [(x_at, zsel) for zsel in range(2) for x_at in (x, x - d, x + d, x + 2)]
    for slab, (x_at, zsel) in zip(slabs, places):
        row = 2 * lax.rem(x_at + 8, XS) + lax.rem(z + zsel, 2)
        step = lax.rem(row - y + 8, ROWS)
        column = jnp.where(step < 3, step, jnp.where(step < 5, step + 3, step - 2)) * 4 * BLK
        place(xs_ref, column, slab, row, 4, pattern_ref, at_ref)
    rest_ref[...] = xs_ref[:, 24 * BLK:]
    right = jnp.concatenate([piece[...] for piece in pieces], axis=0)
    out_ref[...] = jnp.dot(xs_ref[:, :24 * BLK], right, preferred_element_type=jnp.float32)


def early(at, pattern, keep, slabs, pieces):
    return pl.pallas_call(
        early_kernel,
        out_shape=(
            jax.ShapeDtypeStruct((512, 512), jnp.float32),
            jax.ShapeDtypeStruct((512, 1024), jnp.bfloat16),
            jax.ShapeDtypeStruct((24,), jnp.int32),
        ),
        in_specs=[SMEM] * 3 + [VMEM] * 14,
        out_specs=(VMEM, VMEM, SMEM),
        scratch_shapes=[pltpu.VMEM((512, 4096), jnp.bfloat16)],
        compiler_params=pltpu.CompilerParams(vmem_limit_bytes=16 * 2**20),
        cost_estimate=pl.CostEstimate(flops=2 * 512 * 3072 * 512, bytes_accessed=4 * 2**20, transcendentals=0),
        name="early",
    )(at, pattern, keep, *slabs, *pieces)


def kept(spots_ref, part):
    places = [spots_ref[part * 8 + i] for i in range(8)]
    spots = [pl.ds(pl.multiple_of(jnp.maximum(p, 0) * BLK, BLK), BLK) for p in places]
    return [p >= 0 for p in places], spots


def late_kernel(shift, spots_ref, s3_ref, s4_ref, rest_ref, sum_ref, out_ref):
    part = lax.rem(spots_ref[16] + shift, 2)
    lines = pl.ds(pl.multiple_of(part * 2 * BLK, 2 * BLK), 2 * BLK)
    right = jnp.concatenate([s3_ref[...], s4_ref[...]], axis=0)
    value = sum_ref[lines, :] + jnp.dot(rest_ref[lines, :], right, preferred_element_type=jnp.float32)
    flags, spots = kept(spots_ref, part)
    for i, (flag, spot) in enumerate(zip(flags, spots)):
        a, b = i // 4, i % 4

        @pl.when(flag)
        def _():
            out_ref[spot, :] = value[a * BLK:(a + 1) * BLK, b * BLK:(b + 1) * BLK]


def late(shift, *arrays):
    return pl.pallas_call(
        functools.partial(late_kernel, shift),
        out_shape=jax.ShapeDtypeStruct((KEPT * BLK, BLK), jnp.float32),
        in_specs=[SMEM] + [VMEM] * 4,
        out_specs=VMEM,
        compiler_params=pltpu.CompilerParams(vmem_limit_bytes=8 * 2**20),
        cost_estimate=pl.CostEstimate(flops=2 * 256 * 1024 * 512, bytes_accessed=2**20, transcendentals=0),
    )(*arrays)


def finish_kernel(spots_ref, own_ref, got_ref, out_ref):
    flags, spots = kept(spots_ref, spots_ref[16])
    for i, (flag, spot) in enumerate(zip(flags, spots)):
        a, b = i // 4, i % 4
        total = jnp.where(flag, own_ref[spot, :] + got_ref[spot, :], 0.0)
        out_ref[a * BLK:(a + 1) * BLK, b * BLK:(b + 1) * BLK] = total.astype(jnp.bfloat16)


def finish(spots, own, got):
    return pl.pallas_call(
        finish_kernel,
        out_shape=jax.ShapeDtypeStruct((2 * BLK, 4 * BLK), jnp.bfloat16),
        in_specs=[SMEM, VMEM, VMEM],
        out_specs=VMEM,
        compiler_params=pltpu.CompilerParams(vmem_limit_bytes=8 * 2**20),
        cost_estimate=pl.CostEstimate(flops=2**20, bytes_accessed=2 * 2**20, transcendentals=0),
        name="finish",
    )(spots, own, got)


def body(sign_iterate, square, pattern, keep):
    l = lax.axis_index("layer")
    y = lax.axis_index("row")
    c = lax.axis_index("col")
    half, part = l // 2, l % 2
    at = jnp.stack([y, c // 4, (c // 2) % 2, c % 2, l, c]).astype(jnp.int32)
    at, sign_iterate, square = lax.optimization_barrier((at, sign_iterate, square))

    def step(value, pairs):
        return lax.ppermute(value, AXES, pairs)

    def down(value, shift):
        return step(value, table(lambda r, x, z, k, l: (r + shift, x, z, k, l)))

    def slab(rows):
        return lax.dynamic_slice(sign_iterate, (rows * 512, part * 256), (512, 256))

    s0 = lax.dynamic_index_in_dim(square.reshape(2, 2, 256, 512), part, 1, False).reshape(512, 512)
    s7 = down(s0, 1)
    z_own = step(slab(1 - half), ACROSS_Z)
    s1 = down(s0, -1)
    x0 = both_cores(slab(half))
    x1 = step(x0, ALONG_X)
    s6 = down(s7, 1)
    z0 = both_cores(z_own)
    z1 = step(z0, ALONG_X)
    s2 = down(s1, -1)
    s5 = down(s6, 1)
    x2 = step(x1, ALONG_X)
    z2 = step(z1, ALONG_X)
    s3 = down(s2, -1)
    s4 = down(s5, 1)
    x1o = step(x1, OTHER_CORE)
    z1o = step(z1, OTHER_CORE)
    slabs = (x0, x1, x1o, x2, z0, z1, z1o, z2)
    total, rest, spots = early(at, pattern, keep, slabs, (s0, s1, s2, s5, s6, s7))
    sent = late(1, spots, s3, s4, rest, total)
    got = step(sent, table(lambda r, x, z, k, l: (r, x, z, k, l ^ 1)))
    own = late(0, spots, s3, s4, rest, total)
    return finish(spots, own, got)


def solution(mesh):
    return jax.shard_map(
        body,
        mesh=mesh,
        in_specs=(P("row", "col"), P("row", "col"), P(), P()),
        out_specs=P(("row", "layer"), "col"),
        check_vma=False,
    )
```
